32 devices in a mesh: aux: 4 (over x, core), orb: 8 (over z, y).
Axes of the slice: x: 2, y: 2, z: 4, core: 2. Of those that a mesh axis runs over, the one named last changes fastest.
Arguments:
- three_center: bfloat16 [640, 8, 3, 4096], P(('aux', 'orb')), may hold values from -1.5 to 1.5
- atom_size: int32 [8], replicated, may hold values from 32 to 64
- tensor_pattern: int32 [40, 8, 3], P('aux', 'orb'), may hold values 0 or 1
- green_occ: bfloat16 [8, 3, 4096], P('orb'), may hold values from -0.5 to 0.5
- green_virt: bfloat16 [8, 3, 4096], P('orb'), may hold values from -0.5 to 0.5
- green_pattern: int32 [8, 3], P('orb'), may hold values 0 or 1
Outputs:
- chi: float32 [640, 640], P(('aux', 'orb'))
The draws below stay inside these ranges and needn't reach their ends.
Inputs may be any that keep to these rules, and one draw needn't show every extreme that they name: `atom_size`: functions in use per block.
All inputs are finite; a program needn't handle non-finite values. No bound on the sum of `tensor_pattern` or of `green_pattern` on one device may be relied on, other than what follows from the above.
Results may differ from the reference program's by a relative error of at most 0.0041.
Values may be sent and summed in bfloat16 or wider, within the bound.
A program may use at most 128 MiB of HBM per device.

```python
import jax
import jax.numpy as jnp
from jax import lax

BS = 64
R = 1
W = 3
ABS = 16
AUX_DEV = 160
NAUX = 640
NOB = 8
NAB = 40
N_AUX = 4


def set_ends(drawn, key, low, largest):
    dims = drawn.shape
    spot = [jax.random.randint(jax.random.fold_in(key, axis), (), 0, dims[axis]) for axis in range(len(dims))]
    drawn = drawn.at[tuple(spot)].set(low)
    longest = dims.index(max(dims))
    spot[longest] = (spot[longest] + 1) % dims[longest]
    return drawn.at[tuple(spot)].set(largest)


def strengthened(entries, key, source, target, shards_of, factor):
    owner, partner = [(jnp.arange(entries.shape[position]) // (entries.shape[position] // shards_of)).reshape([-1 if axis == position else 1 for axis in range(entries.ndim)]) for position in (source, target)]
    chosen = jax.random.permutation(key, shards_of)[partner]
    strong = (owner == chosen) | (owner == (partner + shards_of // 2) % shards_of)
    return jnp.where(strong, factor * entries, entries)


def block_levels(key, shape, split, least, largest):
    level, own = 1.0, jax.random.fold_in(key, 6)
    for axis_at, parts in split:
        steps = jnp.exp(jax.random.uniform(jax.random.fold_in(own, axis_at), (parts,), jnp.float32, least / len(split), largest / len(split)))
        level = level * jnp.repeat(steps, shape[axis_at] // parts).reshape([-1 if axis == axis_at else 1 for axis in range(len(shape))])
    return level


def gaussian(key, extent, width, most, pieces=(), kind=jnp.bfloat16):
    values = jax.random.normal(key, extent, jnp.float32) * width
    if len(pieces) > 0:
        values = block_levels(key, extent, pieces, -0.22, 0.18) * values
    return jnp.clip(values, min=-most, max=most).astype(kind)


def bell_draw_with(stream_key, shape, spread, limit, split, heavy, kind=jnp.bfloat16):
    drawn = spread * jax.random.normal(stream_key, shape, jnp.float32)
    if split:
        drawn = drawn * block_levels(stream_key, shape, split, -0.22, 0.18)
    return jnp.clip(strengthened(drawn, jax.random.fold_in(stream_key, 3), *heavy), -limit, limit).astype(kind)


def setup_inputs(seed: int = 0) -> dict:
    splits = jax.random.split(jax.random.key(seed), 7)
    three_center = bell_draw_with(splits[0], (NAUX, NOB, W, BS * BS), ((NOB * BS * BS) ** -0.25), 1.5, ((0, 32),), (1, 0, 8, 2.0))
    atom_size = set_ends(jax.random.randint(splits[1], (NOB,), BS // 2, BS + 1), jax.random.fold_in(splits[1], 1), BS // 2, BS).astype(jnp.int32)
    tensor_pattern = set_ends((jax.random.randint(splits[2], (NAB, NOB, W), 0, 4) < 3).astype(jnp.int32), jax.random.fold_in(splits[2], 1), 0, 1)
    green_occ = gaussian(splits[3], (NOB, W, BS * BS), (2 * BS) ** -0.5, 0.5, ((0, 8),))
    green_virt = gaussian(splits[4], (NOB, W, BS * BS), (2 * BS) ** -0.5, 0.5, ((0, 8),))
    green_pattern = set_ends((jax.random.randint(splits[5], (NOB, W), 0, 4) < 3).astype(jnp.int32), jax.random.fold_in(splits[5], 1), 0, 1)
    return dict(three_center=three_center, atom_size=atom_size, tensor_pattern=tensor_pattern, green_occ=green_occ, green_virt=green_virt, green_pattern=green_pattern)


def block_masks(atom_size, first_block, local_blocks):
    total_blocks = atom_size.shape[0]
    owned = first_block + jnp.arange(local_blocks, dtype=jnp.int32)
    offsets = jnp.arange(W, dtype=jnp.int32)
    partner = owned[:, None] + offsets[None, :] - R
    inside = (partner >= 0) & (partner < total_blocks)
    catalog = jnp.arange(total_blocks, dtype=jnp.int32)
    size_partner = jnp.sum(jnp.where(partner[:, :, None] == catalog, atom_size, 0), axis=2)
    size_owned = jnp.sum(jnp.where(owned[:, None] == catalog, atom_size, 0), axis=1)
    funcs = jnp.arange(BS, dtype=jnp.int32)
    rows_ok = (funcs[None, None, :] < size_partner[:, :, None]) & inside[:, :, None]
    cols_ok = funcs[None, :] < size_owned[:, None]
    pair_ok = rows_ok[:, :, :, None] & cols_ok[:, None, None, :]
    return inside, pair_ok.reshape(local_blocks, W, BS * BS)


def first_products(padded_occ, tensor):
    rows = tensor.shape[0]
    local_blocks = tensor.shape[1]
    results = []
    for target in range(W):
        total = jnp.zeros((rows, local_blocks, BS, BS), jnp.float32)
        for source in range(W):
            if abs(target - source) <= R:
                green = padded_occ[source:source + local_blocks, target - source + R].reshape(local_blocks, BS, BS)
                block = tensor[:, :, source].reshape(rows, local_blocks, BS, BS)
                total = total + jnp.einsum("nlm,pnmv->pnlv", green.astype(jnp.float32), block.astype(jnp.float32))
        results.append(total.reshape(rows, local_blocks, BS * BS))
    return jnp.stack(results, axis=2).astype(jnp.bfloat16)


def second_products(padded_tensor, virt):
    rows = padded_tensor.shape[0]
    local_blocks = virt.shape[0]
    results = []
    for target in range(W):
        total = jnp.zeros((rows, local_blocks, BS, BS), jnp.float32)
        for source in range(W):
            if abs(target - source) <= R:
                block = padded_tensor[:, source:source + local_blocks, target - source + R].reshape(rows, local_blocks, BS, BS)
                green = virt[:, source].reshape(local_blocks, BS, BS)
                total = total + jnp.einsum("pnls,nsv->pnlv", block.astype(jnp.float32), green.astype(jnp.float32))
        results.append(total.reshape(rows, local_blocks, BS * BS))
    return jnp.stack(results, axis=2).astype(jnp.bfloat16)


def reference(three_center, atom_size, tensor_pattern, green_occ, green_virt, green_pattern):
    inside, pair_ok = block_masks(atom_size, jnp.int32(0), NOB)
    pattern_rows = jnp.repeat(tensor_pattern, ABS, axis=0)
    keep = (pattern_rows[..., None] > 0) & pair_ok[None]
    tensor = jnp.where(keep, three_center, jnp.zeros((), three_center.dtype))
    diagonal = jnp.arange(W, dtype=jnp.int32) == R
    green_keep = ((green_pattern > 0) | diagonal[None, :]) & inside
    green_mask = green_keep[..., None] & pair_ok
    occ = jnp.where(green_mask, green_occ, jnp.zeros((), green_occ.dtype))
    virt = jnp.where(green_mask, green_virt, jnp.zeros((), green_virt.dtype))
    padded_occ = jnp.pad(occ, ((R, R), (0, 0), (0, 0)))
    groups = tensor.reshape(N_AUX, AUX_DEV, NOB, W, BS * BS)

    def second_group(group):
        return second_products(jnp.pad(group, ((0, 0), (R, R), (0, 0), (0, 0))), virt)

    second = lax.map(second_group, groups).reshape(NAUX, NOB * W * BS * BS)

    def chi_group(group):
        first = first_products(padded_occ, group).reshape(AUX_DEV, NOB * W * BS * BS)
        return lax.dot_general(first, second, (((1,), (1,)), ((), ())), preferred_element_type=jnp.float32)

    return lax.map(chi_group, groups).reshape(NAUX, NAUX)
```

```python
import functools

import jax
import jax.numpy as jnp
from jax import lax
from jax.experimental import pallas as pl
from jax.experimental.pallas import tpu as pltpu
from jax.sharding import PartitionSpec as P

BS = 64
R = 1
W = 3
ABS = 16
LANES = 128


def block_masks(atom_size, first_block, local_blocks):
    total_blocks = atom_size.shape[0]
    owned = first_block + jnp.arange(local_blocks, dtype=jnp.int32)
    offsets = jnp.arange(W, dtype=jnp.int32)
    partner = owned[:, None] + offsets[None, :] - R
    inside = (partner >= 0) & (partner < total_blocks)
    catalog = jnp.arange(total_blocks, dtype=jnp.int32)
    size_partner = jnp.sum(jnp.where(partner[:, :, None] == catalog, atom_size, 0), axis=2)
    size_owned = jnp.sum(jnp.where(owned[:, None] == catalog, atom_size, 0), axis=1)
    funcs = jnp.arange(BS, dtype=jnp.int32)
    rows_ok = (funcs[None, None, :] < size_partner[:, :, None]) & inside[:, :, None]
    cols_ok = funcs[None, :] < size_owned[:, None]
    pair_ok = rows_ok[:, :, :, None] & cols_ok[:, None, None, :]
    return (inside, pair_ok.reshape(local_blocks, W, BS * BS))


def gather(x, axis):
    count = lax.axis_size(axis)
    return lax.all_to_all(
        jnp.broadcast_to(x[None], (count,) + x.shape), axis, split_axis=0, concat_axis=0, tiled=True
    )


def x_kernel(t_ref, v_ref, o_ref, x_ref, second_ref):
    n = pl.program_id(0)
    blocks = t_ref.shape[0]
    width = t_ref.shape[3]
    tiles = width // LANES
    for e in range(W):
        total = None
        for d in range(W):
            if abs(e - d) <= R:
                m = jnp.clip(n + d - R, 0, blocks - 1)
                block = t_ref[m, e - d + R]
                rows = jnp.concatenate(
                    [block[:, j * LANES : (j + 1) * LANES] for j in range(tiles)], axis=0
                )
                part = jnp.dot(rows, v_ref[0, d], preferred_element_type=jnp.float32)
                total = part if total is None else total + part
        total = total.astype(second_ref.dtype)
        for j in range(tiles):
            second_ref[e * BS : (e + 1) * BS, j * LANES : (j + 1) * LANES] = total[
                j * BS : (j + 1) * BS
            ]
    x_ref[0] = jnp.dot(o_ref[0], second_ref[...], preferred_element_type=jnp.float32).astype(
        x_ref.dtype
    )


def x_products(tensor, virt2, occ_t):
    blocks, _, _, width = tensor.shape
    depth = W * BS
    return pl.pallas_call(
        x_kernel,
        grid=(blocks,),
        in_specs=[
            pl.BlockSpec(tensor.shape, lambda n: (0, 0, 0, 0)),
            pl.BlockSpec((1, W, LANES, LANES), lambda n: (n, 0, 0, 0)),
            pl.BlockSpec((1, depth, depth), lambda n: (n, 0, 0)),
        ],
        out_specs=pl.BlockSpec((1, depth, width), lambda n: (n, 0, 0)),
        out_shape=jax.ShapeDtypeStruct((blocks, depth, width), jnp.bfloat16),
        scratch_shapes=[pltpu.VMEM((depth, width), jnp.bfloat16)],
        cost_estimate=pl.CostEstimate(
            flops=blocks * width * (7 * BS * LANES * 2 + depth * depth * 2),
            bytes_accessed=tensor.size * 4,
            transcendentals=0,
        ),
    )(tensor, virt2, occ_t)


def body(three_center, atom_size, tensor_pattern, green_occ, green_virt, green_pattern):
    both = ("aux", "orb")
    n_aux, n_orb = lax.axis_size("aux"), lax.axis_size("orb")
    aux, orb = lax.axis_index("aux"), lax.axis_index("orb")
    rows, blocks = three_center.shape[0], three_center.shape[1]
    local_blocks = green_occ.shape[0]
    depth = local_blocks * W * BS * BS
    share = depth // n_aux
    width = rows * BS

    outgoing = three_center.reshape(rows, n_orb, n_aux, share).transpose(2, 1, 0, 3)
    outgoing = outgoing.reshape(n_aux * n_orb, rows, share)
    incoming = lax.all_to_all(outgoing, both, split_axis=0, concat_axis=0, tiled=True)

    inside, pair_ok = block_masks(atom_size, orb * local_blocks, local_blocks)
    diagonal = jnp.arange(W, dtype=jnp.int32) == R
    green_keep = ((green_pattern > 0) | diagonal[None, :]) & inside
    green_mask = green_keep[..., None] & pair_ok
    occ = jnp.where(green_mask, green_occ, jnp.zeros((), green_occ.dtype))
    virt = jnp.where(green_mask, green_virt, jnp.zeros((), green_virt.dtype))
    pattern = (tensor_pattern > 0).astype(jnp.bfloat16)
    groups = pattern.shape[0]
    packed = jnp.concatenate([occ.reshape(-1), virt.reshape(-1), pattern.reshape(-1)])
    gathered = gather(packed, "orb")
    size = local_blocks * W * BS * BS
    occ_all = gathered[:, :size].reshape(blocks, W, BS, BS)
    virt_all = gathered[:, size : 2 * size].reshape(blocks, W, BS, BS)
    pattern_orb = gathered[:, 2 * size :].reshape(n_orb, groups, local_blocks, W)
    pattern_orb = pattern_orb.transpose(1, 0, 2, 3).reshape(groups, blocks, W)
    pattern_aux = gather(pattern, "aux").reshape(n_aux * groups, local_blocks, W)

    _, pair_all = block_masks(atom_size, jnp.int32(0), blocks)
    rows_here = jnp.repeat(pattern_orb, ABS, axis=0)
    rows_here = lax.dynamic_slice_in_dim(rows_here, orb * rows, rows, axis=0)
    pair_all = pair_all.reshape(blocks, W, BS, BS)
    turned = three_center.reshape(rows, blocks, W, BS, BS).transpose(1, 2, 3, 0, 4)
    keep = (rows_here.transpose(1, 2, 0)[:, :, None, :, None] > 0) & pair_all[:, :, :, None, :]
    tensor = jnp.where(keep, turned, jnp.zeros((), turned.dtype)).reshape(blocks, W, BS, width)
    zero = jnp.zeros_like(virt_all)
    virt2 = jnp.concatenate(
        [jnp.concatenate([virt_all, zero], axis=3), jnp.concatenate([zero, virt_all], axis=3)],
        axis=2,
    )
    occ_pad = jnp.pad(occ_all, ((R, R), (0, 0), (0, 0), (0, 0)))
    none = jnp.zeros((blocks, BS, BS), occ_all.dtype)
    occ_t = jnp.concatenate(
        [
            jnp.concatenate(
                [
                    occ_pad[d : d + blocks, e - d + R].transpose(0, 2, 1)
                    if abs(e - d) <= R
                    else none
                    for e in range(W)
                ],
                axis=2,
            )
            for d in range(W)
        ],
        axis=1,
    )
    x = x_products(tensor, virt2, occ_t)
    x = x.reshape(n_orb, n_aux, share // BS, rows, BS).transpose(1, 0, 3, 2, 4)
    x = x.reshape(n_aux * n_orb, rows, share)
    right = lax.all_to_all(x, both, split_axis=0, concat_axis=0, tiled=True)
    right = right.reshape(n_aux * n_orb * rows, share)

    ok = lax.dynamic_slice_in_dim(pair_ok.reshape(depth), aux * share, share, axis=0)
    full = jnp.broadcast_to(
        pattern_aux.reshape(n_aux * groups, local_blocks * W, 1),
        (n_aux * groups, local_blocks * W, BS * BS),
    ).reshape(n_aux * groups, depth)
    held = lax.dynamic_slice_in_dim(full, aux * share, share, axis=1)
    held = jnp.repeat(held, ABS, axis=0)
    left = incoming.reshape(n_aux * n_orb * rows, share)
    left = jnp.where((held > 0) & ok[None], left, jnp.zeros((), left.dtype))

    part = lax.dot_general(
        left, right, (((1,), (1,)), ((), ())), preferred_element_type=jnp.float32
    )
    functions = part.shape[0]
    part = part.astype(jnp.bfloat16).reshape(n_aux, functions // n_aux, functions)
    part = lax.all_to_all(part, "aux", split_axis=0, concat_axis=0, tiled=True)
    part = jnp.sum(part.astype(jnp.float32), axis=0).astype(jnp.bfloat16)
    part = part.reshape(n_orb, rows, functions)
    part = lax.all_to_all(part, "orb", split_axis=0, concat_axis=0, tiled=True)
    return jnp.sum(part.astype(jnp.float32), axis=0)


def solution(mesh):
    return jax.shard_map(
        body,
        mesh=mesh,
        in_specs=(
            P(("aux", "orb"), None, None, None),
            P(),
            P("aux", "orb", None),
            P("orb", None, None),
            P("orb", None, None),
            P("orb", None),
        ),
        out_specs=P(("aux", "orb"), None),
        check_vma=False,
    )
```

```python
import functools

import jax
import jax.numpy as jnp
from jax import lax
from jax.experimental import pallas as pl
from jax.experimental.pallas import tpu as pltpu
from jax.sharding import PartitionSpec as P

BS = 64
R = 1
W = 3
ABS = 16
LANES = 128


def block_masks(atom_size, first_block, local_blocks):
    total_blocks = atom_size.shape[0]
    owned = first_block + jnp.arange(local_blocks, dtype=jnp.int32)
    offsets = jnp.arange(W, dtype=jnp.int32)
    partner = owned[:, None] + offsets[None, :] - R
    inside = (partner >= 0) & (partner < total_blocks)
    catalog = jnp.arange(total_blocks, dtype=jnp.int32)
    size_partner = jnp.sum(jnp.where(partner[:, :, None] == catalog, atom_size, 0), axis=2)
    size_owned = jnp.sum(jnp.where(owned[:, None] == catalog, atom_size, 0), axis=1)
    funcs = jnp.arange(BS, dtype=jnp.int32)
    rows_ok = (funcs[None, None, :] < size_partner[:, :, None]) & inside[:, :, None]
    cols_ok = funcs[None, :] < size_owned[:, None]
    pair_ok = rows_ok[:, :, :, None] & cols_ok[:, None, None, :]
    return (inside, pair_ok.reshape(local_blocks, W, BS * BS))


def gather(x, axis):
    count = lax.axis_size(axis)
    return lax.all_to_all(
        jnp.broadcast_to(x[None], (count,) + x.shape), axis, split_axis=0, concat_axis=0, tiled=True
    )


def x_kernel(t_ref, v_ref, o_ref, x_ref, second_ref):
    n = pl.program_id(0)
    blocks = t_ref.shape[0]
    width = t_ref.shape[3]
    tiles = width // LANES
    for e in range(W):
        total = None
        for d in range(W):
            if abs(e - d) <= R:
                m = jnp.clip(n + d - R, 0, blocks - 1)
                block = t_ref[m, e - d + R]
                rows = jnp.concatenate(
                    [block[:, j * LANES : (j + 1) * LANES] for j in range(tiles)], axis=0
                )
                part = jnp.dot(rows, v_ref[0, d], preferred_element_type=jnp.float32)
                total = part if total is None else total + part
        total = total.astype(second_ref.dtype)
        for j in range(tiles):
            second_ref[e * BS : (e + 1) * BS, j * LANES : (j + 1) * LANES] = total[
                j * BS : (j + 1) * BS
            ]
    x_ref[0] = jnp.dot(o_ref[0], second_ref[...], preferred_element_type=jnp.float32).astype(
        x_ref.dtype
    )


def x_products(tensor, virt2, occ_t):
    blocks, _, _, width = tensor.shape
    depth = W * BS
    return pl.pallas_call(
        x_kernel,
        grid=(blocks,),
        in_specs=[
            pl.BlockSpec(tensor.shape, lambda n: (0, 0, 0, 0)),
            pl.BlockSpec((1, W, LANES, LANES), lambda n: (n, 0, 0, 0)),
            pl.BlockSpec((1, depth, depth), lambda n: (n, 0, 0)),
        ],
        out_specs=pl.BlockSpec((1, depth, width), lambda n: (n, 0, 0)),
        out_shape=jax.ShapeDtypeStruct((blocks, depth, width), jnp.bfloat16),
        scratch_shapes=[pltpu.VMEM((depth, width), jnp.bfloat16)],
        cost_estimate=pl.CostEstimate(
            flops=blocks * width * (7 * BS * LANES * 2 + depth * depth * 2),
            bytes_accessed=tensor.size * 4,
            transcendentals=0,
        ),
    )(tensor, virt2, occ_t)


def send_kernel(share, first, t_ref, pair_ref, row_ref, out_ref):
    blocks = t_ref.shape[1]
    size = t_ref.shape[3]
    targets = out_ref.shape[0]
    for n in range(blocks):
        for d in range(W):
            b = n * W + d
            begin, end = max(b * size, first), min((b + 1) * size, first + targets * share)
            if begin >= end:
                continue
            kept = row_ref[:, b : b + 1] * pair_ref[b : b + 1, :]
            block = t_ref[:, n, d, :] * kept
            while begin < end:
                target = (begin - first) // share
                stop = min(end, first + (target + 1) * share)
                at = begin - first - target * share
                out_ref[target, :, at : at + stop - begin] = block[
                    :, begin - b * size : stop - b * size
                ]
                begin = stop


def send_layout(three_center, pair, row, targets, share, first):
    rows = three_center.shape[0]
    return pl.pallas_call(
        functools.partial(send_kernel, share, first),
        in_specs=[pl.BlockSpec(memory_space=pltpu.VMEM)] * 3,
        out_specs=pl.BlockSpec(memory_space=pltpu.VMEM),
        out_shape=jax.ShapeDtypeStruct((targets, rows, share), jnp.bfloat16),
        compiler_params=pltpu.CompilerParams(vmem_limit_bytes=48 << 20),
    )(three_center, pair, row)


def chi_kernel(left_ref, right_ref, out_ref, l_ref, r_ref):
    sources, rows, _ = right_ref.shape
    for s in range(sources):
        l_ref[s * rows : (s + 1) * rows, :] = left_ref[s]
        r_ref[s * rows : (s + 1) * rows, :] = right_ref[s]
    out_ref[...] = lax.dot_general(
        l_ref[...], r_ref[...], (((1,), (1,)), ((), ())), preferred_element_type=jnp.float32
    ).astype(out_ref.dtype)


def chi_part(left, right):
    sources, rows, share = right.shape
    functions = sources * rows
    return pl.pallas_call(
        chi_kernel,
        in_specs=[pl.BlockSpec(memory_space=pltpu.VMEM)] * 2,
        out_specs=pl.BlockSpec(memory_space=pltpu.VMEM),
        out_shape=jax.ShapeDtypeStruct((functions, functions), jnp.bfloat16),
        scratch_shapes=[pltpu.VMEM((functions, share), jnp.bfloat16)] * 2,
        compiler_params=pltpu.CompilerParams(vmem_limit_bytes=56 << 20),
    )(left, right)


def body(three_center, atom_size, tensor_pattern, green_occ, green_virt, green_pattern):
    both = ("aux", "orb")
    n_aux, n_orb = lax.axis_size("aux"), lax.axis_size("orb")
    orb = lax.axis_index("orb")
    rows, blocks = three_center.shape[0], three_center.shape[1]
    local_blocks = green_occ.shape[0]
    area = BS * BS
    targets = n_aux * n_orb
    width = rows * BS
    total = blocks * W * area
    trim = area if (total - 2 * area) % (targets * LANES) == 0 else 0
    share = (total - 2 * trim) // targets

    inside, pair_ok = block_masks(atom_size, orb * local_blocks, local_blocks)
    diagonal = jnp.arange(W, dtype=jnp.int32) == R
    green_keep = ((green_pattern > 0) | diagonal[None, :]) & inside
    green_mask = green_keep[..., None] & pair_ok
    occ = jnp.where(green_mask, green_occ, jnp.zeros((), green_occ.dtype))
    virt = jnp.where(green_mask, green_virt, jnp.zeros((), green_virt.dtype))
    pattern = (tensor_pattern > 0).astype(jnp.bfloat16)
    groups = pattern.shape[0]
    pattern_orb = gather(pattern, "orb").transpose(1, 0, 2, 3).reshape(groups, blocks * W)
    greens = jnp.concatenate([occ, virt], axis=1)

    _, pair_all = block_masks(atom_size, jnp.int32(0), blocks)
    pair_all = pair_all.reshape(blocks * W, area).astype(jnp.bfloat16)
    rows_here = jnp.repeat(pattern_orb, ABS, axis=0)
    rows_here = lax.dynamic_slice_in_dim(rows_here, orb * rows, rows, axis=0)
    outgoing = send_layout(three_center, pair_all, rows_here, targets, share, trim)
    left = lax.all_to_all(outgoing, both, split_axis=0, concat_axis=0, tiled=True)

    gathered = gather(greens, "orb").reshape(blocks, 2 * W, BS, BS)
    occ_all, virt_all = gathered[:, :W], gathered[:, W:]

    turned = outgoing.reshape(targets, rows, share // BS, BS).transpose(0, 2, 1, 3)
    tensor = turned.reshape(targets * share // BS, width)
    tensor = jnp.pad(tensor, ((trim // BS, trim // BS), (0, 0))).reshape(blocks, W, BS, width)
    zero = jnp.zeros_like(virt_all)
    virt2 = jnp.concatenate(
        [jnp.concatenate([virt_all, zero], axis=3), jnp.concatenate([zero, virt_all], axis=3)],
        axis=2,
    )
    occ_pad = jnp.pad(occ_all, ((R, R), (0, 0), (0, 0), (0, 0)))
    none = jnp.zeros((blocks, BS, BS), occ_all.dtype)
    occ_t = jnp.concatenate(
        [
            jnp.concatenate(
                [
                    occ_pad[d : d + blocks, e - d + R].transpose(0, 2, 1)
                    if abs(e - d) <= R
                    else none
                    for e in range(W)
                ],
                axis=2,
            )
            for d in range(W)
        ],
        axis=1,
    )
    x = x_products(tensor, virt2, occ_t).reshape(total // BS, width)
    x = x[trim // BS : (total - trim) // BS]
    x = x.reshape(targets, share // BS, rows, BS).transpose(0, 2, 1, 3).reshape(targets, rows, share)
    right = lax.all_to_all(x, both, split_axis=0, concat_axis=0, tiled=True)

    part = chi_part(left, right)
    functions = part.shape[0]
    part = part.reshape(n_aux, functions // n_aux, functions)
    part = lax.all_to_all(part, "aux", split_axis=0, concat_axis=0, tiled=True)
    part = jnp.sum(part.astype(jnp.float32), axis=0).astype(jnp.bfloat16)
    part = part.reshape(n_orb, rows, functions)
    part = lax.all_to_all(part, "orb", split_axis=0, concat_axis=0, tiled=True)
    return jnp.sum(part.astype(jnp.float32), axis=0)


def solution(mesh):
    return jax.shard_map(
        body,
        mesh=mesh,
        in_specs=(
            P(("aux", "orb"), None, None, None),
            P(),
            P("aux", "orb", None),
            P("orb", None, None),
            P("orb", None, None),
            P("orb", None),
        ),
        out_specs=P(("aux", "orb"), None),
        check_vma=False,
    )
```

```python
import functools

import jax
import jax.numpy as jnp
from jax import lax
from jax.experimental import pallas as pl
from jax.experimental.pallas import tpu as pltpu
from jax.sharding import PartitionSpec as P

BS = 64
R = 1
W = 3
ABS = 16
LANES = 128


def block_masks(atom_size, first_block, local_blocks):
    total_blocks = atom_size.shape[0]
    owned = first_block + jnp.arange(local_blocks, dtype=jnp.int32)
    offsets = jnp.arange(W, dtype=jnp.int32)
    partner = owned[:, None] + offsets[None, :] - R
    inside = (partner >= 0) & (partner < total_blocks)
    catalog = jnp.arange(total_blocks, dtype=jnp.int32)
    size_partner = jnp.sum(jnp.where(partner[:, :, None] == catalog, atom_size, 0), axis=2)
    size_owned = jnp.sum(jnp.where(owned[:, None] == catalog, atom_size, 0), axis=1)
    funcs = jnp.arange(BS, dtype=jnp.int32)
    rows_ok = (funcs[None, None, :] < size_partner[:, :, None]) & inside[:, :, None]
    cols_ok = funcs[None, :] < size_owned[:, None]
    pair_ok = rows_ok[:, :, :, None] & cols_ok[:, None, None, :]
    return (inside, pair_ok.reshape(local_blocks, W, BS * BS))


def gather(x, axis):
    count = lax.axis_size(axis)
    return lax.all_to_all(
        jnp.broadcast_to(x[None], (count,) + x.shape), axis, split_axis=0, concat_axis=0, tiled=True
    )


def x_kernel(t_ref, v_ref, o_ref, x_ref, second_ref):
    n = pl.program_id(0)
    blocks = t_ref.shape[0]
    width = t_ref.shape[3]
    tiles = width // LANES
    for e in range(W):
        total = None
        for d in range(W):
            if abs(e - d) <= R:
                m = jnp.clip(n + d - R, 0, blocks - 1)
                block = t_ref[m, e - d + R]
                rows = jnp.concatenate(
                    [block[:, j * LANES : (j + 1) * LANES] for j in range(tiles)], axis=0
                )
                part = jnp.dot(rows, v_ref[0, d], preferred_element_type=jnp.float32)
                total = part if total is None else total + part
        total = total.astype(second_ref.dtype)
        for j in range(tiles):
            second_ref[e * BS : (e + 1) * BS, j * LANES : (j + 1) * LANES] = total[
                j * BS : (j + 1) * BS
            ]
    x_ref[0] = jnp.dot(o_ref[0], second_ref[...], preferred_element_type=jnp.float32).astype(
        x_ref.dtype
    )


def x_products(tensor, virt2, occ_t):
    blocks, _, _, width = tensor.shape
    depth = W * BS
    return pl.pallas_call(
        x_kernel,
        grid=(blocks,),
        in_specs=[
            pl.BlockSpec(tensor.shape, lambda n: (0, 0, 0, 0)),
            pl.BlockSpec((1, W, LANES, LANES), lambda n: (n, 0, 0, 0)),
            pl.BlockSpec((1, depth, depth), lambda n: (n, 0, 0)),
        ],
        out_specs=pl.BlockSpec((1, depth, width), lambda n: (n, 0, 0)),
        out_shape=jax.ShapeDtypeStruct((blocks, depth, width), jnp.bfloat16),
        scratch_shapes=[pltpu.VMEM((depth, width), jnp.bfloat16)],
        cost_estimate=pl.CostEstimate(
            flops=blocks * width * (7 * BS * LANES * 2 + depth * depth * 2),
            bytes_accessed=tensor.size * 4,
            transcendentals=0,
        ),
    )(tensor, virt2, occ_t)


def send_kernel(share, first, t_ref, pair_ref, row_ref, out_ref):
    blocks = t_ref.shape[2]
    size = t_ref.shape[3]
    targets = out_ref.shape[0]
    for n in range(blocks):
        for d in range(W):
            b = n * W + d
            begin, end = max(b * size, first), min((b + 1) * size, first + targets * share)
            if begin >= end:
                continue
            kept = row_ref[:, b : b + 1] * pair_ref[b : b + 1, :]
            block = t_ref[:, d, n, :] * kept
            while begin < end:
                target = (begin - first) // share
                stop = min(end, first + (target + 1) * share)
                at = begin - first - target * share
                out_ref[target, :, at : at + stop - begin] = block[
                    :, begin - b * size : stop - b * size
                ]
                begin = stop


def send_layout(three_center, pair, row, targets, share, first):
    rows = three_center.shape[0]
    return pl.pallas_call(
        functools.partial(send_kernel, share, first),
        in_specs=[pl.BlockSpec(memory_space=pltpu.VMEM)] * 3,
        out_specs=pl.BlockSpec(memory_space=pltpu.VMEM),
        out_shape=jax.ShapeDtypeStruct((targets, rows, share), jnp.bfloat16),
        compiler_params=pltpu.CompilerParams(vmem_limit_bytes=48 << 20),
    )(three_center.transpose(0, 2, 1, 3), pair, row)


def chi_kernel(left_ref, right_ref, out_ref, l_ref, r_ref):
    sources, rows, _ = right_ref.shape
    for s in range(sources):
        l_ref[s * rows : (s + 1) * rows, :] = left_ref[s]
        r_ref[s * rows : (s + 1) * rows, :] = right_ref[s]
    out_ref[...] = lax.dot_general(
        l_ref[...], r_ref[...], (((1,), (1,)), ((), ())), preferred_element_type=jnp.float32
    ).astype(out_ref.dtype)


def chi_part(left, right):
    sources, rows, share = right.shape
    functions = sources * rows
    return pl.pallas_call(
        chi_kernel,
        in_specs=[pl.BlockSpec(memory_space=pltpu.VMEM)] * 2,
        out_specs=pl.BlockSpec(memory_space=pltpu.VMEM),
        out_shape=jax.ShapeDtypeStruct((functions, functions), jnp.bfloat16),
        scratch_shapes=[pltpu.VMEM((functions, share), jnp.bfloat16)] * 2,
        compiler_params=pltpu.CompilerParams(vmem_limit_bytes=56 << 20),
    )(left, right)


def body(three_center, atom_size, tensor_pattern, green_occ, green_virt, green_pattern):
    both = ("aux", "orb")
    n_aux, n_orb = lax.axis_size("aux"), lax.axis_size("orb")
    orb = lax.axis_index("orb")
    rows, blocks = three_center.shape[0], three_center.shape[1]
    local_blocks = green_occ.shape[0]
    area = BS * BS
    targets = n_aux * n_orb
    width = rows * BS
    total = blocks * W * area
    trim = area if (total - 2 * area) % (targets * LANES) == 0 else 0
    share = (total - 2 * trim) // targets

    groups = tensor_pattern.shape[0]
    flags = jnp.concatenate([tensor_pattern.reshape(-1), green_pattern.reshape(-1)])
    flags = (flags > 0).astype(jnp.bfloat16)
    counts = (groups * local_blocks * W, local_blocks * W)
    lines = -(-flags.shape[0] // area)
    flags = jnp.pad(flags, (0, lines * area - flags.shape[0])).reshape(lines, area)
    packed = jnp.concatenate(
        [green_occ.reshape(-1, area), green_virt.reshape(-1, area), flags], axis=0
    )
    packed = gather(packed, "orb")
    flags = packed[:, 2 * local_blocks * W :].reshape(n_orb, lines * area)
    pattern_orb = flags[:, : counts[0]].reshape(n_orb, groups, local_blocks, W)
    pattern_orb = pattern_orb.transpose(1, 0, 2, 3).reshape(groups, blocks * W)
    green_all = flags[:, counts[0] : counts[0] + counts[1]].reshape(blocks, W)

    inside, pair_ok = block_masks(atom_size, jnp.int32(0), blocks)
    pair_all = pair_ok.reshape(blocks * W, area).astype(jnp.bfloat16)
    rows_here = jnp.repeat(pattern_orb, ABS, axis=0)
    rows_here = lax.dynamic_slice_in_dim(rows_here, orb * rows, rows, axis=0)
    outgoing = send_layout(three_center, pair_all, rows_here, targets, share, trim)
    left = lax.all_to_all(outgoing, both, split_axis=0, concat_axis=0, tiled=True)

    diagonal = jnp.arange(W, dtype=jnp.int32) == R
    green_keep = ((green_all > 0) | diagonal[None, :]) & inside
    green_mask = (green_keep[..., None] & pair_ok).reshape(blocks, W, BS, BS)
    half = local_blocks * W
    occ_all = packed[:, :half].reshape(blocks, W, BS, BS)
    virt_all = packed[:, half : 2 * half].reshape(blocks, W, BS, BS)
    occ_all = jnp.where(green_mask, occ_all, jnp.zeros((), occ_all.dtype))
    virt_all = jnp.where(green_mask, virt_all, jnp.zeros((), virt_all.dtype))

    turned = outgoing.reshape(targets, rows, share // BS, BS).transpose(0, 2, 1, 3)
    tensor = turned.reshape(targets * share // BS, width)
    tensor = jnp.pad(tensor, ((trim // BS, trim // BS), (0, 0))).reshape(blocks, W, BS, width)
    zero = jnp.zeros_like(virt_all)
    virt2 = jnp.concatenate(
        [jnp.concatenate([virt_all, zero], axis=3), jnp.concatenate([zero, virt_all], axis=3)],
        axis=2,
    )
    occ_pad = jnp.pad(occ_all, ((R, R), (0, 0), (0, 0), (0, 0)))
    none = jnp.zeros((blocks, BS, BS), occ_all.dtype)
    occ_t = jnp.concatenate(
        [
            jnp.concatenate(
                [
                    occ_pad[d : d + blocks, e - d + R].transpose(0, 2, 1)
                    if abs(e - d) <= R
                    else none
                    for e in range(W)
                ],
                axis=2,
            )
            for d in range(W)
        ],
        axis=1,
    )
    x = x_products(tensor, virt2, occ_t).reshape(total // BS, width)
    x = x[trim // BS : (total - trim) // BS]
    x = x.reshape(targets, share // BS, rows, BS).transpose(0, 2, 1, 3).reshape(targets, rows, share)
    right = lax.all_to_all(x, both, split_axis=0, concat_axis=0, tiled=True)

    part = chi_part(left, right)
    functions = part.shape[0]
    part = part.reshape(n_aux, functions // n_aux, functions)
    part = lax.all_to_all(part, "aux", split_axis=0, concat_axis=0, tiled=True)
    part = jnp.sum(part.astype(jnp.float32), axis=0).astype(jnp.bfloat16)
    part = part.reshape(n_orb, rows, functions)
    part = lax.all_to_all(part, "orb", split_axis=0, concat_axis=0, tiled=True)
    return jnp.sum(part.astype(jnp.float32), axis=0)


def solution(mesh):
    return jax.shard_map(
        body,
        mesh=mesh,
        in_specs=(
            P(("aux", "orb"), None, None, None),
            P(),
            P("aux", "orb", None),
            P("orb", None, None),
            P("orb", None, None),
            P("orb", None),
        ),
        out_specs=P(("aux", "orb"), None),
        check_vma=False,
    )
```
